256 devices in a mesh: vol: 64 (over x, z, core), slab: 4 (over y).
Axes of the slice: x: 4, y: 4, z: 8, core: 2. Of those that a mesh axis runs over, the one named last changes fastest.
Arguments:
- face_disp: bfloat16 [64, 524288], P(None, ('vol', 'slab')), may hold values from -6 to 6
- contact_owner: int32 [524288, 1], P(('vol', 'slab')), may hold values from 0 to 63; in each aligned block of 2048 rows (0 to 2047, 2048 to 4095, ...) at most 128 rows name the same one
- segment: int32 [524288], P(('vol', 'slab')), may hold values from 0 to 7
- face_area: float32 [524288], P(('vol', 'slab')), may hold values from 0.5 to 5
- face_nodes: int32 [4, 524288], P(None, ('vol', 'slab')), may hold values from 0 to 1023
- mortar_blocks: bfloat16 [2048, 64, 64], P(('vol', 'slab')), may hold values from -0.75 to 0.75
- gap_offset: bfloat16 [2048, 64], P(('vol', 'slab')), may hold values from -6 to 6
- shape_table: float32 [12, 64], replicated, may hold values from -0.75 to 0.75
- node_disp: float32 [3, 262144], P(None, ('vol', 'slab')), may hold values from -6 to 6
- stiffness: float32 [262144], P(('vol', 'slab')), may hold values from 0.2 to 2
- connect: int32 [8, 262144], P(None, ('vol', 'slab')), may hold values from 0 to 1023
- elem_matrix: float32 [24, 24], replicated, may hold values from -1.25 to 1.25
Outputs:
- residual: float32 [3, 262144], P(None, ('vol', 'slab'))
The draws below stay inside these ranges and needn't reach their ends.
Inputs may be any that keep to these rules, and one draw needn't show every extreme that they name: `contact_owner`: in each block of 2048 faces no owner index is named by more than 128 faces, and some owner index is named by exactly 128.
All inputs are finite; a program needn't handle non-finite values.
Results may differ from the reference program's by a relative error of at most 0.0028.
Values may be sent and summed in bfloat16 or wider, within the bound.
A program may use at most 64 MiB of HBM per device.

```python
import math
import jax
import jax.numpy as jnp
import numpy as np
from jax import lax

K = 64
F_DEV = 2048
G = 8
NODE_DEV = 1024
SH = 256
CAP = 128
FACES = 524288
SEGS = 2048
NODES = 262144
ELEMS = 262144
N_VOL = 64
N_SLAB = 4


def set_ends(entries, rng, least, top_value):
    place = [jax.random.randint(jax.random.fold_in(rng, axis), (), 0, length) for axis, length in enumerate(entries.shape)]
    widest = entries.shape.index(max(entries.shape))
    neighbour = place[:widest] + [(place[widest] + 1) % entries.shape[widest]] + place[widest + 1:]
    return entries.at[tuple(place)].set(least).at[tuple(neighbour)].set(top_value)


def block_scale(key, dims, cuts, least, high):
    loudness, own = 1.0, jax.random.fold_in(key, 6)
    for dim, shards_of in cuts:
        heights = jnp.exp(jax.random.uniform(jax.random.fold_in(own, dim), (shards_of,), jnp.float32, least / len(cuts), high / len(cuts)))
        loudness = loudness * jnp.repeat(heights, dims[dim] // shards_of).reshape([-1 if axis == dim else 1 for axis in range(len(dims))])
    return loudness


def assign_block(stream_key, own, number, rows, number_of, top, limit, lean):
    sequence = jax.random.permutation(stream_key, number_of)
    crowded, ordinary = load_shares(number_of, rows * top, limit, lean, True), load_shares(number_of, rows * top, limit, lean, False)
    places = jnp.arange(number_of)

    def named(sizes, turn):
        used = int((sizes > 0).sum())
        fixed = max(1, used // 4)
        passed = fixed + (places - fixed + turn * (used - fixed)) % max(1, number_of - fixed)
        return jnp.zeros((number_of,), jnp.int32).at[sequence[jnp.where(places < fixed, places, passed)]].set(jnp.asarray(sizes, jnp.int32))

    sizes = jnp.where(number % 4 == 0, named(crowded, number // 4), named(ordinary, number - number // 4 - 1))
    mixed = jax.random.permutation(jax.random.fold_in(own, 3), number_of)
    source_of, receiver = mixed[0:number_of // 2 * 2:2], mixed[1:number_of // 2 * 2:2]
    room = jnp.minimum(sizes[source_of] - 1, limit - sizes[receiver]) // 2
    room = jnp.where((source_of == sequence[0]) | (receiver == sequence[0]) | (sizes[receiver] == 0), 0, jnp.maximum(room, 0))
    passed = jax.random.randint(jax.random.fold_in(own, 4), (number_of // 2,), 0, 1 << 20) % (room + 1)
    sizes = sizes.at[source_of].add(-passed).at[receiver].add(passed)
    members = jnp.searchsorted(jnp.cumsum(sizes), jnp.arange(rows * top), side="right").astype(jnp.int32)
    listing = members.reshape(top, rows).T
    listing = listing[jax.random.permutation(jax.random.fold_in(own, 1), rows)]
    turn = jax.random.randint(jax.random.fold_in(own, 2), (rows, 1), 0, top)
    return jnp.take_along_axis(listing, (jnp.arange(top)[None, :] + turn) % top, axis=1)


def load_shares(amount, total, reach, lean, full):
    portions = [(1 << 20) // math.isqrt(grade ** lean) + 1 for grade in range(1, amount + 1)]
    largest = reach if full else min(reach, max(-(-total // amount), total * portions[0] // sum(portions)))
    least = 1 if total - largest >= amount - 1 else 0
    given, surplus = [largest] + [least] * (amount - 1), total - largest - least * (amount - 1)
    while surplus > 0:
        candidates = [i for i in range(1, amount) if given[i] < largest] or [i for i in range(1, amount) if given[i] < reach]
        pool, remaining = sum([portions[i] for i in candidates]), surplus
        for i in candidates:
            more = min(reach - given[i], max(1, remaining * portions[i] // pool), surplus)
            given[i] = given[i] + more
            surplus = surplus - more
    return np.array(given)


def normal_values(own_key, shape, scale, most, cuts=(), held_as=jnp.bfloat16):
    values = jax.random.normal(own_key, shape, jnp.float32) * scale
    if len(cuts) > 0:
        values = block_scale(own_key, shape, cuts, -0.22, 0.18) * values
    return jnp.clip(values, min=-most, max=most).astype(held_as)


def setup_inputs(seed: int = 0) -> dict:
    streams_of = jax.random.split(jax.random.key(seed), 13)
    face_disp = normal_values(streams_of[0], (K, FACES), 1.0, 6.0, ((1, 256),))
    contact_owner_keys = jax.random.split(jax.random.fold_in(streams_of[1], 1), FACES // F_DEV)
    contact_owner_turns = jax.random.permutation(jax.random.fold_in(streams_of[1], 3), FACES // F_DEV)
    contact_owner = jax.vmap(lambda own, number: assign_block(jax.random.fold_in(streams_of[1], 2), own, number, F_DEV, N_VOL, 1, CAP, 2))(contact_owner_keys, contact_owner_turns).reshape((FACES, 1))
    segment = set_ends(jax.random.randint(streams_of[2], (FACES,), 0, G), jax.random.fold_in(streams_of[2], 1), 0, G - 1).astype(jnp.int32)
    face_area = jnp.clip(jnp.exp(math.log(5.0) - 2.3025851 * jax.random.uniform(streams_of[3], (FACES,), jnp.float32) ** block_scale(streams_of[3], (FACES,), ((0, 256),), -0.2, 0.2)), 0.5, 5.0)
    face_nodes = set_ends(jax.random.randint(streams_of[4], (4, FACES), 0, NODE_DEV), jax.random.fold_in(streams_of[4], 1), 0, NODE_DEV - 1).astype(jnp.int32)
    mortar_blocks = normal_values(streams_of[5], (SEGS, K, K), K ** -0.5, 0.75, ((0, 256),))
    gap_offset = normal_values(streams_of[6], (SEGS, K), 1.0, 6.0, ((0, 256),))
    shape_table = normal_values(streams_of[7], (12, K), K ** -0.5, 0.75, (), jnp.float32)
    node_disp = normal_values(streams_of[8], (3, NODES), 1.0, 6.0, ((1, 256),), jnp.float32)
    stiffness = jnp.clip(jnp.exp(math.log(2.0) - 2.3025851 * jax.random.uniform(streams_of[9], (ELEMS,), jnp.float32) ** block_scale(streams_of[9], (ELEMS,), ((0, 256),), -0.2, 0.2)), 0.2, 2.0)
    connect = set_ends(jax.random.randint(streams_of[10], (8, ELEMS), 0, NODE_DEV), jax.random.fold_in(streams_of[10], 1), 0, NODE_DEV - 1).astype(jnp.int32)
    elem_matrix = normal_values(streams_of[11], (24, 24), 24 ** -0.5, 1.25, (), jnp.float32)
    return dict(face_disp=face_disp, contact_owner=contact_owner, segment=segment, face_area=face_area, face_nodes=face_nodes, mortar_blocks=mortar_blocks, gap_offset=gap_offset, shape_table=shape_table, node_disp=node_disp, stiffness=stiffness, connect=connect, elem_matrix=elem_matrix)


highest = lax.Precision.HIGHEST


def reference(face_disp, contact_owner, segment, face_area, face_nodes, mortar_blocks, gap_offset, shape_table, node_disp, stiffness, connect, elem_matrix):
    device_count = N_VOL * N_SLAB
    face_block = jnp.arange(FACES, dtype=jnp.int32) // F_DEV
    slab_of = face_block % N_SLAB
    target = ((contact_owner[:, 0] * N_SLAB + slab_of) * G + segment).astype(jnp.int32)

    def by_device(array, row_count):
        return array.reshape(row_count, device_count, -1).transpose(1, 0, 2)

    def face_group(pieces):
        disp_block, target_block = pieces
        chosen = jnp.take(mortar_blocks, target_block, axis=0).astype(jnp.float32)
        offsets = jnp.take(gap_offset, target_block, axis=0).astype(jnp.float32).T
        gap = jnp.einsum("fij,jf->if", chosen, disp_block.astype(jnp.float32), precision=highest) - offsets
        traction = jax.nn.softplus(-gap)
        return jnp.einsum("fij,if->jf", chosen, traction, precision=highest).astype(jnp.bfloat16)

    seg_force = lax.map(face_group, (by_device(face_disp, K), target.reshape(device_count, F_DEV)))
    seg_force = seg_force.transpose(1, 0, 2).reshape(K, FACES)
    face_force = seg_force.astype(jnp.float32) * face_area[None, :]
    nodal_twelve = jnp.dot(shape_table, face_force, precision=highest, preferred_element_type=jnp.float32)

    def block_residual(pieces):
        node_block, conn_block, stiff_block, fnode_block, nodal_block = pieces
        elem_count = conn_block.shape[1]
        node_count = node_block.shape[1]
        face_count = fnode_block.shape[1]
        elem_disp = jnp.take(node_block, conn_block, axis=1).transpose(1, 0, 2).reshape(24, elem_count)
        elem_force = stiff_block[None, :] * jnp.dot(elem_matrix, elem_disp, precision=highest, preferred_element_type=jnp.float32)
        spread = elem_force.reshape(8, 3, elem_count).transpose(1, 0, 2).reshape(3, 8 * elem_count)
        internal = jnp.zeros((3, node_count), jnp.float32).at[:, conn_block.reshape(-1)].add(spread)
        pressed = nodal_block.reshape(4, 3, face_count).transpose(1, 0, 2).reshape(3, 4 * face_count)
        contact = jnp.zeros((3, node_count), jnp.float32).at[:, fnode_block.reshape(-1)].add(pressed)
        return internal - contact

    pieces = (by_device(node_disp, 3), by_device(connect, 8), stiffness.reshape(device_count, -1), by_device(face_nodes, 4), by_device(nodal_twelve, 12))
    unsummed = lax.map(block_residual, pieces)
    grid = unsummed.reshape(N_VOL, N_SLAB, 3, NODE_DEV)
    zero_rim = jnp.zeros((N_VOL, 1, 3, SH), jnp.float32)
    from_below = jnp.concatenate([zero_rim, grid[:, :-1, :, NODE_DEV - SH:]], axis=1)
    from_above = jnp.concatenate([grid[:, 1:, :, :SH], zero_rim], axis=1)
    lower = grid[:, :, :, :SH] + from_below
    upper = grid[:, :, :, NODE_DEV - SH:] + from_above
    summed = jnp.concatenate([lower, grid[:, :, :, SH:NODE_DEV - SH], upper], axis=3)
    return summed.transpose(2, 0, 1, 3).reshape(3, NODES)
```

```python
import functools

import jax
import jax.numpy as jnp
from jax import lax
from jax.experimental import pallas as pl
from jax.experimental.pallas import tpu as pltpu
from jax.sharding import PartitionSpec as P

SH = 256
TILE = 32
GROUP = 4
F32, BF16, I32 = jnp.float32, jnp.bfloat16, jnp.int32
NT = (((1,), (1,)), ((), ()))


def dot(a, b):
    return jnp.dot(a, b, preferred_element_type=F32)


def dot_nt(a, b):
    return lax.dot_general(a, b, NT, preferred_element_type=F32)


def iota(shape, dim):
    return lax.broadcasted_iota(I32, shape, dim)


def hot(mask):
    return jnp.where(mask, 1.0, 0.0).astype(BF16)


def split(value):
    high = value.astype(BF16)
    return high, (value - high.astype(F32)).astype(BF16)


def sort_faces(owner, owners):
    faces = owner.shape[1]
    member = iota((owners, faces), 0) == owner
    member_low = hot(member)
    upto = hot(iota((256, 256), 0) <= iota((256, 256), 1))
    carry = jnp.zeros((owners, 1), F32)
    parts = []
    for k in range(faces // 256):
        part = dot(member_low[:, 256 * k : 256 * k + 256], upto) + carry
        carry = part[:, 255:256]
        parts.append(part)
    rank = jnp.concatenate(parts, axis=1)
    before = hot(iota((owners, owners), 1) < iota((owners, owners), 0))
    count = jnp.broadcast_to(carry, (owners, 128))
    first = dot(before, count.astype(BF16))
    row = jnp.sum(jnp.where(member, rank - 1.0 + first[:, 0:1], 0.0), axis=0, keepdims=True)
    return row.astype(I32), count, first, before


def tile_table(count, first, before):
    owners = count.shape[0]
    tiles = jnp.floor((count + (TILE - 1)) * (1.0 / TILE))
    begin = dot(before, tiles.astype(BF16))
    place = iota((owners, 128), 1).astype(F32)
    inside = (place >= begin) & (place < begin + tiles)
    ids = iota((owners, 128), 0).astype(F32)
    owner = jnp.sum(jnp.where(inside, ids, 0.0), axis=0, keepdims=True)
    start = jnp.sum(jnp.where(inside, first + TILE * (place - begin), 0.0), axis=0, keepdims=True)
    total = jnp.sum(tiles, axis=0, keepdims=True)
    lane = iota((1, 128), 1).astype(F32)
    start = jnp.where(lane < total, start, 2048.0)
    rest = jnp.zeros((5, 128), F32)
    return jnp.concatenate([owner, start, total, rest], axis=0).astype(I32)


def permute(row, disp, segment, area, nodes, sorted_ref):
    faces = row.shape[1]
    nodes_high = nodes >> 7
    area_a = area.astype(BF16)
    area_b, area_c = split(area - area_a.astype(F32))
    extra = jnp.concatenate([(nodes - (nodes_high << 7)).astype(F32), nodes_high.astype(F32)], axis=0).astype(BF16)
    content = jnp.concatenate(
        [
            disp,
            extra,
            area_a,
            area_b,
            area_c,
            jnp.zeros((53, faces), BF16),
            jnp.broadcast_to(segment.astype(F32), (128, faces)).astype(BF16),
        ],
        axis=0,
    )
    for k in range(faces // 256):
        pick = hot(iota((256, faces), 0) + 256 * k == row)
        sorted_ref[256 * k : 256 * k + 256, :] = dot_nt(pick, content)


def high_hot(high_row):
    return iota((8, high_row.shape[1]), 0) == high_row


def elements(node, connect, stiffness, matrix, total_ref, low_ref):
    count = connect.shape[1]
    rows = []
    for c in range(3):
        grid = jnp.concatenate([node[c : c + 1, 128 * h : 128 * h + 128] for h in range(8)], axis=0)
        high, low = split(grid)
        rows += [high.astype(F32), low.astype(F32)]
    table = jnp.concatenate(rows, axis=0).astype(BF16)
    picked, highs = [], []
    for a in range(8):
        index = connect[a : a + 1, :]
        high = index >> 7
        low = hot(iota((128, count), 0) == index - (high << 7))
        low_ref[a] = low
        mask = high_hot(high)
        highs.append(mask)
        got = dot(table, low)
        picked.append(jnp.concatenate([jnp.where(mask, got[8 * i : 8 * i + 8], 0.0) for i in range(6)], axis=0).astype(BF16))
    spread = hot(iota((24, 384), 1) // 16 == iota((24, 384), 0))
    m_high, m_low = split(matrix)
    wide = jnp.concatenate([dot(m_high, spread), dot(m_low, spread)], axis=0).astype(BF16)
    force = dot(wide, jnp.concatenate(picked, axis=0))
    force = (force[:24] + force[24:]) * stiffness
    total = jnp.zeros((48, 128), F32)
    for a in range(8):
        parts = []
        for c in range(3):
            for part in split(force[3 * a + c : 3 * a + c + 1]):
                parts.append(jnp.where(highs[a], part.astype(F32), 0.0))
        total = total + dot_nt(jnp.concatenate(parts, axis=0).astype(BF16), low_ref[a])
    total_ref[...] = total


def scatter_faces(nodal, low_rows, high_rows, total):
    count = nodal.shape[1]
    for a in range(4):
        low = hot(iota((128, count), 0) == low_rows[a : a + 1])
        mask = high_hot(high_rows[a : a + 1])
        parts = []
        for c in range(3):
            for part in split(nodal[3 * a + c : 3 * a + c + 1]):
                parts.append(jnp.where(mask, part.astype(F32), 0.0))
        total = total - dot_nt(jnp.concatenate(parts, axis=0).astype(BF16), low)
    return total


def segment_masks(segment):
    half = (iota(segment.shape, 1) >= 64).astype(F32)
    return [segment - half == 2.0 * p for p in range(4)]


def contact(meta_ref, blocks_ref, sorted_ref, segment_ref, gap_ref, force_ref):
    steps = (meta_ref[2, 0] + (GROUP - 1)) // GROUP

    def gap_step(i, _):
        for k in range(GROUP):
            t = i * GROUP + k
            owner, start = meta_ref[0, t], meta_ref[1, t]
            disp = sorted_ref[pl.ds(start, TILE), :].astype(BF16)[:, 0:64]
            masks = segment_masks(segment_ref[pl.ds(start, TILE), :])
            every = dot(disp, blocks_ref[owner, 0:64, :])
            offset = blocks_ref[owner, 64:72, :].astype(F32)[0:1]
            gap = jnp.zeros((TILE, 128), F32)
            for p in range(4):
                at = slice(128 * p, 128 * p + 128)
                gap = jnp.where(masks[p], every[:, at] - offset[:, at], gap)
            gap_ref[pl.ds(start, TILE), :] = gap
        return 0

    lax.fori_loop(0, steps, gap_step, 0)
    gap = gap_ref[0:2048]
    gap_ref[0:2048] = jnp.maximum(-gap, 0.0) + jnp.log(1.0 + jnp.exp(-jnp.abs(gap)))

    def force_step(i, _):
        for k in range(GROUP):
            t = i * GROUP + k
            owner, start = meta_ref[0, t], meta_ref[1, t]
            traction = gap_ref[pl.ds(start, TILE), :]
            masks = segment_masks(segment_ref[pl.ds(start, TILE), :])
            high, low = split(traction)
            high, low = high.astype(F32), low.astype(F32)
            spread = jnp.concatenate(
                [jnp.concatenate([jnp.where(m, part, 0.0) for m in masks], axis=1) for part in (high, low)], axis=0
            ).astype(BF16)
            force = dot_nt(spread, blocks_ref[owner, 0:64, :])
            force = force[:TILE] + force[TILE:]
            force_ref[pl.ds(start, TILE), :] = jnp.concatenate([force, jnp.zeros_like(force)], axis=1)
        return 0

    lax.fori_loop(0, steps, force_step, 0)


NX, NZ = 4, 8
MESH = pl.DeviceIdType.MESH
BLOCK = 72
A, B = (0, 32), (32, 40)
A0, A1, B0, B1 = (0, 16), (16, 16), (32, 24), (56, 16)


def sign(d):
    return "+" if d > 0 else "-"


def transfers():
    t = []

    def add(*entry):
        t.append(entry)

    for d in (1, -1):
        add("aX" + sign(d), ("x", d), 0, 0, A, ())
        add("aZ1_0" + sign(d), ("z", d), 0, 0, A, ())
        add("bZ1" + sign(d), ("z", d), 0, 0, B, ())
        add("bX0" + sign(d), ("x", d), 0, 0, B, ())
    add("so", ("s", 1), 0, 0, B, ())
    add("aX2+", ("x", 1), -1, 0, A0, ("aX+",))
    add("aX2-", ("x", -1), 1, 0, A1, ("aX-",))
    src = {0: (), -1: ("aX+",), 1: ("aX-",), 2: ("aX2+", "aX2-")}
    for d in (1, -1):
        q = sign(d)
        for rx in (-1, 1, 2):
            add(f"aZ1_{rx}" + q, ("z", d), rx, 0, A, src[rx])
        for k in (2, 3):
            for rx in (0, -1, 1, 2):
                add(f"aZ{k}_{rx}" + q, ("z", d), rx, -(k - 1) * d, A, (f"aZ{k - 1}_{rx}" + q,))
        for rx in (0, 2) if d > 0 else (-1, 1):
            add(f"aZ4_{rx}" + q, ("z", d), rx, -3 * d, A, (f"aZ3_{rx}" + q,))
        add("bZ2" + q, ("z", d), 0, -d, B, ("bZ1" + q,))
        add("bZ3" + q, ("z", d), 0, -2 * d, B, ("bZ2" + q,))
        add("bZ4" + q, ("z", d), 0, -3 * d, B0 if d > 0 else B1, ("bZ3" + q,))
    came = {0: (), -1: ("bZ1+",), 1: ("bZ1-",), -2: ("bZ2+",), 2: ("bZ2-",), -3: ("bZ3+",), 3: ("bZ3-",), 4: ("bZ4+", "bZ4-")}
    for rz in (-1, 1, -2, 2, -3, 3, 4):
        for d in (1, -1):
            add(f"bX{rz}" + sign(d), ("x", d), 0, rz, B, came[rz])
    for rz in (0, -1, 1, -2, 2, -3, 3, 4):
        d = 1 if rz in (0, 1, 2, 3) else -1
        add(f"bY{rz}", ("x", d), -d, rz, B, (f"bX{rz}" + sign(d),))
    add("s_x", ("s", 1), None, 0, A, ("aX+", "aX-", "aX2+", "aX2-"))
    for d in (1, -1):
        q = sign(d)
        for k in (1, 2, 3):
            add(f"sz{k}" + q, ("s", 1), None, -k * d, A, tuple(f"aZ{k}_{rx}" + q for rx in (0, -1, 1, 2)))
    add("sz4", ("s", 1), None, 4, A, ("aZ4_0+", "aZ4_2+", "aZ4_-1-", "aZ4_1-"))
    for rz in (-1, 1, -2, 2, -3, 3, 4):
        add(f"sb{rz}", ("s", 1), 0, rz, B, came[rz])
    for rz in (0, -1, 1, -2, 2, -3, 3, 4):
        add(f"sx{rz}p", ("s", 1), -1, rz, B, (f"bX{rz}+",))
        add(f"sx{rz}m", ("s", 1), 1, rz, B, (f"bX{rz}-",))
        add(f"sx{rz}f", ("s", 1), 2, rz, B, (f"bY{rz}",))
    return t


COPIES = len(transfers())
ORDER = [0, 1, 2, 3, 4, 5, 6, 7, 8, -1, 9, 11, 27, -5, 10, 12, 28, -4, 57, 80, -2, 14, -8, 81, -6, 30, -10, -3, 24, 43, 44, 73, -7, 40, 45, 46, 74, -11, 13, 29, 65, -58, 82, -12, 15, -28, 31, -13, 16, -29, 32, -15, 18, -45, 58, 84, -44, 83, -31, 34, -47, 87, -25, 25, 47, 48, 75, -46, 59, 86, -41, 41, 49, 50, 76, -14, 17, 66, -30, 33, 69, -16, 19, -59, 85, -32, 35, -48, 89, -17, 20, -33, 36, -49, 60, 90, -19, 22, -35, -60, 88, -51, 93, -26, 26, 51, 52, 77, -50, 61, 92, -42, 42, 53, 54, 78, -18, 21, 67, -34, 37, 70, -20, -61, 91, -36, 38, -23, -52, 95, -53, 62, 96, -21, -37, 39, -62, 94, -27, -43, 55, 56, 79, -55, 99, -54, 63, 98, -22, 23, 68, -38, 71, -63, 97, -39, -57, 64, 102, -40, -56, 101, -64, 100, -24, 72, -65, 103, -9, -81, -82, -74, -75, -66, -83, -85, -84, -76, -88, -87, -77, -67, -70, -90, -86, -91, -89, -94, -78, -93, -79, -68, -71, -92, -96, -97, -95, -100, -80, -99, -69, -98, -72, -101, -103, -102, -73, -104]


class Gather:
    def __init__(self, mine, blocks, send_sem, recv_sem):
        self.mine, self.blocks, self.send_sem, self.recv_sem = mine, blocks, send_sem, recv_sem
        v, self.y = lax.axis_index("vol"), lax.axis_index("slab")
        self.v, self.x, self.z, self.c = v, v // 16, (v // 2) % NZ, v % 2
        self.table = transfers()

    def device(self, direction):
        kind, d = direction
        if kind == "x":
            return (((self.x + d + NX) % NX * NZ + self.z) * 2 + self.c, self.y)
        if kind == "z":
            return ((self.x * NZ + (self.z + d + NZ) % NZ) * 2 + self.c, self.y)
        return (self.v + 1 - 2 * self.c, self.y)

    def at(self, rx, rz, core, rows):
        xs = slice(None) if rx is None else (self.x + rx + NX) % NX
        return self.blocks.at[xs, (self.z + rz + NZ) % NZ, core, pl.ds(*rows)]

    def copy(self, i, arriving=False):
        _, direction, rx, rz, rows, after = self.table[i]
        kind, d = direction
        if arriving:
            rx = rx - d if kind == "x" else rx
            rz = rz - d if kind == "z" else rz
            source = target = self.at(rx, rz, 1 - self.c if kind == "s" else self.c, rows)
        else:
            target = self.at(rx, rz, self.c, rows)
            source = target if after else self.mine.at[pl.ds(*rows)]
        return pltpu.make_async_remote_copy(
            src_ref=source, dst_ref=target, send_sem=self.send_sem.at[i], recv_sem=self.recv_sem.at[i],
            device_id=self.device(direction), device_id_type=MESH)

    def greet(self):
        barrier = pltpu.get_barrier_semaphore()
        for direction in (("x", 1), ("x", -1), ("z", 1), ("z", -1), ("s", 1)):
            pl.semaphore_signal(barrier, inc=1, device_id=self.device(direction), device_id_type=MESH)
        return lambda: pl.semaphore_wait(barrier, 5)

    def run(self, events):
        for e in events:
            if e >= 0:
                self.copy(e).start()
            else:
                self.copy(~e, True).wait_recv()

    def leave(self):
        for i in range(COPIES):
            self.copy(i).wait_send()


ANY = pl.BlockSpec(memory_space=pl.ANY)
VM = pl.BlockSpec(memory_space=pltpu.VMEM)
SM = pl.BlockSpec(memory_space=pltpu.SMEM)


def kernel_a(*refs):
    inputs, outputs, buffers = refs[:11], refs[11:15], refs[15:26]
    mine, low_ref, load_sem, own_sem, send_sem, recv_sem = refs[26:]
    blocks_ref, sorted_ref, meta_ref, total_ref = outputs
    gather = Gather(mine, blocks_ref, send_sem, recv_sem)
    enter = gather.greet()
    loads = [pltpu.make_async_copy(s, d, load_sem.at[k]) for k, (s, d) in enumerate(zip(inputs, buffers))]
    for load in loads:
        load.start()
    mortar, offset, owner, disp, segment, area, nodes, node, stiffness, connect, matrix = buffers
    loads[0].wait()
    loads[1].wait()
    eye = hot(iota((64, 64), 0) == iota((64, 64), 1))
    mine[0:64, :] = dot_nt(eye, mortar[...].reshape(512, 64)).astype(BF16)
    gaps = offset[...].astype(F32)
    line = jnp.concatenate([gaps[g : g + 1] for g in range(8)], axis=1)
    mine[64:72, :] = jnp.broadcast_to(line, (8, 512)).astype(BF16)
    own = pltpu.make_async_copy(mine, gather.at(0, 0, gather.c, (0, BLOCK)), own_sem)
    own.start()
    enter()
    own.wait()
    gather.run(ORDER[:9])
    for load in loads[2:]:
        load.wait()
    row, count, first, before = sort_faces(owner[...], 64)
    meta_ref[...] = tile_table(count, first, before)
    permute(row, disp[...], segment[...], area[...], nodes[...], sorted_ref)
    elements(node[...], connect[...], stiffness[...], matrix[...], total_ref, low_ref)
    gather.run(ORDER[9:])
    gather.leave()


def stage_a(*arrays):
    return pl.pallas_call(
        kernel_a,
        out_shape=(
            jax.ShapeDtypeStruct((NX, NZ, 2, BLOCK, 512), BF16),
            jax.ShapeDtypeStruct((2048, 256), F32),
            jax.ShapeDtypeStruct((8, 128), I32),
            jax.ShapeDtypeStruct((48, 128), F32),
        ),
        in_specs=[ANY] * 11,
        out_specs=(ANY, VM, VM, VM),
        scratch_shapes=[pltpu.VMEM(a.shape, a.dtype) for a in arrays]
        + [
            pltpu.VMEM((BLOCK, 512), BF16),
            pltpu.VMEM((8, 128, 1024), BF16),
            pltpu.SemaphoreType.DMA((11,)),
            pltpu.SemaphoreType.DMA,
            pltpu.SemaphoreType.DMA((COPIES,)),
            pltpu.SemaphoreType.DMA((COPIES,)),
        ],
        compiler_params=pltpu.CompilerParams(collective_id=0, has_side_effects=True, vmem_limit_bytes=60 << 20),
        name="gather_blocks",
    )(*arrays)


def kernel_b(meta_ref, blocks_in, sorted_in, force_ref, blocks_ref, sorted_ref, segment_ref, gap_ref, out_ref, sem):
    load = pltpu.make_async_copy(blocks_in, blocks_ref, sem)
    load.start()
    sorted_ref[0:2048, :] = sorted_in[:, 0:128]
    segment_ref[0:2048, :] = sorted_in[:, 128:256]
    sorted_ref[2048:, :] = jnp.zeros((TILE, 128), F32)
    segment_ref[2048:, :] = jnp.zeros((TILE, 128), F32)
    load.wait()
    contact(meta_ref, blocks_ref, sorted_ref, segment_ref, gap_ref, out_ref)
    force_ref[...] = out_ref[0:2048, :].astype(BF16)


def stage_b(meta, blocks, rows):
    return pl.pallas_call(
        kernel_b,
        out_shape=jax.ShapeDtypeStruct((2048, 128), BF16),
        in_specs=[SM, ANY, VM],
        out_specs=VM,
        scratch_shapes=[
            pltpu.VMEM((64, BLOCK, 512), BF16),
            pltpu.VMEM((2048 + TILE, 128), F32),
            pltpu.VMEM((2048 + TILE, 128), F32),
            pltpu.VMEM((2048 + TILE, 128), F32),
            pltpu.VMEM((2048 + TILE, 128), F32),
            pltpu.SemaphoreType.DMA,
        ],
        compiler_params=pltpu.CompilerParams(vmem_limit_bytes=48 << 20),
        name="contact_tiles",
    )(meta, blocks.reshape(64, BLOCK, 512), rows)


def finish(rows, force, shape, total):
    choose = hot(iota((16, 128), 1) == iota((16, 128), 0) + 64)
    extra = dot_nt(choose, rows)
    area = extra[8:9] + extra[9:10] + extra[10:11]
    s_high, s_low = split(shape)
    nodal = dot_nt(jnp.concatenate([s_high.astype(F32), s_low.astype(F32)], axis=0).astype(BF16), force)
    nodal = (nodal[:12] + nodal[12:]) * area
    return scatter_faces(nodal, extra[0:4].astype(I32), extra[4:8].astype(I32), total)


def kernel_c(sorted_ref, force_ref, shape_ref, total_ref, out_ref, rims, came, send_sem, recv_sem):
    v, y = lax.axis_index("vol"), lax.axis_index("slab")
    slabs = lax.axis_size("slab")
    up, down = (v, (y + 1) % slabs), (v, (y + slabs - 1) % slabs)
    barrier = pltpu.get_barrier_semaphore()
    for peer in (up, down):
        pl.semaphore_signal(barrier, inc=1, device_id=peer, device_id_type=MESH)
    total = finish(sorted_ref[:, 0:128].astype(BF16), force_ref[:, 0:64], shape_ref[...], total_ref[...])
    grids = [total[16 * c : 16 * c + 8] + total[16 * c + 8 : 16 * c + 16] for c in range(3)]
    for c in range(3):
        rims[8 * c : 8 * c + 8] = grids[c]
    pl.semaphore_wait(barrier, 2)
    copies = [
        pltpu.make_async_remote_copy(
            src_ref=rims, dst_ref=came.at[k], send_sem=send_sem.at[k], recv_sem=recv_sem.at[k], device_id=peer, device_id_type=MESH)
        for k, peer in enumerate((up, down))
    ]
    for copy in copies:
        copy.start()
    for copy in copies:
        copy.wait()
    for c in range(3):
        for h in range(8):
            line = grids[c][h : h + 1]
            if h < 2:
                line = line + jnp.where(y > 0, came[0, 8 * c + h + 6 : 8 * c + h + 7], 0.0)
            if h >= 6:
                line = line + jnp.where(y < slabs - 1, came[1, 8 * c + h - 6 : 8 * c + h - 5], 0.0)
            out_ref[c : c + 1, 128 * h : 128 * h + 128] = line


def stage_c(rows, force, shape, total):
    return pl.pallas_call(
        kernel_c,
        out_shape=jax.ShapeDtypeStruct((3, 1024), F32),
        in_specs=[VM] * 4,
        out_specs=VM,
        scratch_shapes=[
            pltpu.VMEM((24, 128), F32),
            pltpu.VMEM((2, 24, 128), F32),
            pltpu.SemaphoreType.DMA((2,)),
            pltpu.SemaphoreType.DMA((2,)),
        ],
        compiler_params=pltpu.CompilerParams(collective_id=1, has_side_effects=True, vmem_limit_bytes=32 << 20),
        name="faces_and_rims",
    )(rows, force, shape, total)


def shards(face_disp, contact_owner, segment, face_area, face_nodes, mortar_blocks, gap_offset, shape_table, node_disp, stiffness, connect, elem_matrix):
    blocks, rows, meta, total = stage_a(
        mortar_blocks, gap_offset, contact_owner.reshape(1, 2048), face_disp, segment.reshape(1, 2048),
        face_area.reshape(1, 2048), face_nodes, node_disp, stiffness.reshape(1, 1024), connect, elem_matrix)
    force = stage_b(meta, blocks, rows)
    return stage_c(rows, force, shape_table, total)


def solution(mesh):
    both = ("vol", "slab")
    in_specs = (
        P(None, both), P(both, None), P(both), P(both), P(None, both), P(both, None, None), P(both, None), P(),
        P(None, both), P(both), P(None, both), P())
    return jax.shard_map(shards, mesh=mesh, in_specs=in_specs, out_specs=P(None, both), check_vma=False)
```

```python
import functools

import jax
import jax.numpy as jnp
from jax import lax
from jax.experimental import pallas as pl
from jax.experimental.pallas import tpu as pltpu
from jax.sharding import PartitionSpec as P

SH = 256
TILE = 32
CAP = 128
F32, BF16, I32 = jnp.float32, jnp.bfloat16, jnp.int32
NT = (((1,), (1,)), ((), ()))


def dot(a, b):
    return jnp.dot(a, b, preferred_element_type=F32)


def dot_nt(a, b):
    return lax.dot_general(a, b, NT, preferred_element_type=F32)


def iota(shape, dim):
    return lax.broadcasted_iota(I32, shape, dim)


def hot(mask):
    return jnp.where(mask, 1.0, 0.0).astype(BF16)


def split(value):
    high = value.astype(BF16)
    return high, (value - high.astype(F32)).astype(BF16)


def sort_faces(owner, owners):
    faces = owner.shape[1]
    member = iota((owners, faces), 0) == owner
    member_low = hot(member)
    upto = hot(iota((256, 256), 0) <= iota((256, 256), 1))
    carry = jnp.zeros((owners, 1), F32)
    parts = []
    for k in range(faces // 256):
        part = dot(member_low[:, 256 * k : 256 * k + 256], upto) + carry
        carry = part[:, 255:256]
        parts.append(part)
    rank = jnp.concatenate(parts, axis=1)
    before = hot(iota((owners, owners), 1) < iota((owners, owners), 0))
    count = jnp.broadcast_to(carry, (owners, 128))
    first = dot(before, count.astype(BF16))
    row = jnp.sum(jnp.where(member, rank - 1.0 + first[:, 0:1], 0.0), axis=0, keepdims=True)
    return row.astype(I32), count, first


def owner_table(first, count):
    owners = first.shape[0]
    mine = iota((owners, 128), 0) == iota((owners, 128), 1)
    lines = [jnp.sum(jnp.where(mine, value, 0.0), axis=0, keepdims=True) for value in (first, count)]
    return jnp.concatenate(lines + [jnp.zeros((6, 128), F32)], axis=0).astype(I32)


def face_content(disp, segment, area, nodes):
    faces = disp.shape[1]
    nodes_high = nodes >> 7
    area_a = area.astype(BF16)
    area_b, area_c = split(area - area_a.astype(F32))
    extra = jnp.concatenate([(nodes - (nodes_high << 7)).astype(F32), nodes_high.astype(F32)], axis=0).astype(BF16)
    return [
        disp,
        extra,
        area_a,
        area_b,
        area_c,
        jnp.zeros((53, faces), BF16),
        jnp.broadcast_to(segment.astype(F32), (128, faces)).astype(BF16),
    ]


def permute_rows(k, row, content, sorted_ref, segment_ref):
    pick = hot(iota((256, row.shape[1]), 0) + 256 * k == row)
    part = dot_nt(pick, content)
    sorted_ref[256 * k : 256 * k + 256, :] = part[:, 0:128]
    segment_ref[256 * k : 256 * k + 256, :] = part[:, 128:256] - (iota((256, 128), 1) >= 64).astype(F32)


def high_hot(high_row):
    return iota((8, high_row.shape[1]), 0) == high_row


def elements(node, connect, stiffness, matrix, total_ref, low_ref):
    count = connect.shape[1]
    rows = []
    for c in range(3):
        grid = jnp.concatenate([node[c : c + 1, 128 * h : 128 * h + 128] for h in range(8)], axis=0)
        high, low = split(grid)
        rows += [high.astype(F32), low.astype(F32)]
    table = jnp.concatenate(rows, axis=0).astype(BF16)
    picked, highs = [], []
    for a in range(8):
        index = connect[a : a + 1, :]
        high = index >> 7
        low = hot(iota((128, count), 0) == index - (high << 7))
        low_ref[a] = low
        mask = high_hot(high)
        highs.append(mask)
        got = dot(table, low)
        picked.append(jnp.concatenate([jnp.where(mask, got[8 * i : 8 * i + 8], 0.0) for i in range(6)], axis=0).astype(BF16))
    spread = hot(iota((24, 384), 1) // 16 == iota((24, 384), 0))
    m_high, m_low = split(matrix)
    wide = jnp.concatenate([dot(m_high, spread), dot(m_low, spread)], axis=0).astype(BF16)
    force = dot(wide, jnp.concatenate(picked, axis=0))
    force = (force[:24] + force[24:]) * stiffness
    total = jnp.zeros((48, 128), F32)
    for a in range(8):
        parts = []
        for c in range(3):
            for part in split(force[3 * a + c : 3 * a + c + 1]):
                parts.append(jnp.where(highs[a], part.astype(F32), 0.0))
        total = total + dot_nt(jnp.concatenate(parts, axis=0).astype(BF16), low_ref[a])
    total_ref[...] += total


def scatter_faces(nodal, low_rows, high_rows, total):
    count = nodal.shape[1]
    for a in range(4):
        low = hot(iota((128, count), 0) == low_rows[a : a + 1])
        mask = high_hot(high_rows[a : a + 1])
        parts = []
        for c in range(3):
            for part in split(nodal[3 * a + c : 3 * a + c + 1]):
                parts.append(jnp.where(mask, part.astype(F32), 0.0))
        total = total - dot_nt(jnp.concatenate(parts, axis=0).astype(BF16), low)
    return total


def segment_masks(segment):
    return [segment == 2.0 * p for p in range(4)]


NX, NZ = 4, 8
MESH = pl.DeviceIdType.MESH
BLOCK = 72
A, B = (0, 16), (16, 56)
B0, B1 = (16, 24), (40, 32)
RING = (0, -1, 1, -2, 2, -3, 3, 4)


def sign(d):
    return "+" if d > 0 else "-"


def transfers():
    t = []

    def add(*entry):
        t.append(entry)

    for d in (1, -1):
        add("z1" + sign(d), ("z", d), ("one", 0, 0), B, ())
        add("z2" + sign(d), ("z", 2 * d), ("one", 0, 0), B, ())
    for d in (1, -1):
        add("ax" + sign(d), ("x", d), ("one", 0, 0), A, ())
    add("a2", ("x", 2), ("one", 0, 0), A, ())
    for d in (1, -1):
        add("z3" + sign(d), ("z", 2 * d), ("one", 0, -d), B, ("z1" + sign(d),))
        add("z4" + sign(d), ("z", 2 * d), ("one", 0, -2 * d), B0 if d > 0 else B1, ("z2" + sign(d),))
    a_line = ("ax+", "ax-", "a2")
    for d in (1, -1):
        add("az1" + sign(d), ("z", d), ("x_all", 0, 0), A, a_line)
        add("az2" + sign(d), ("z", 2 * d), ("x_all", 0, 0), A, a_line)
    for k in RING:
        for d in (1, -1):
            add(f"x{k}" + sign(d), ("x", d), ("one", 0, k), B, z_arrivals(k))
    for d in (1, -1):
        add("az3" + sign(d), ("z", 2 * d), ("x_all", 0, -d), A, ("az1" + sign(d),))
        add("az4" + sign(d), ("z", 2 * d), ("x_low" if d > 0 else "x_high", 0, -2 * d), A, ("az2" + sign(d),))
    for k in RING:
        d = 1 if k in (0, 1, 2, 3) else -1
        add(f"y{k}", ("x", d), ("one", -d, k), B, (f"x{k}" + sign(d),))
    add("s0", ("s", 1), ("z_all", 0, 0), B, tuple(q for k in RING for q in z_arrivals(k)))
    add("s-1", ("s", 1), ("z_all", -1, 0), B, tuple(f"x{k}+" for k in RING))
    add("s1", ("s", 1), ("z_all", 1, 0), B, tuple(f"x{k}-" for k in RING))
    add("sa", ("s", 1), ("all", 0, 0), A, a_line + tuple(q for k in RING for q in az_arrivals(k)))
    for k in RING:
        add(f"sy{k}", ("s", 1), ("one", 2, k), B, (f"y{k}",))
    return t


def z_arrivals(k):
    if k == 0:
        return ()
    if k == 4:
        return ("z4+", "z4-")
    return (f"z{abs(k)}" + sign(-k),)


def az_arrivals(k):
    return tuple("a" + q for q in z_arrivals(k))


def needed(core, rx, k):
    if core:
        return {"sa"} | ({f"sy{k}"} if rx == 2 else {f"s{rx}"})
    part_a = set(az_arrivals(k)) if k else set({0: (), -1: ("ax+",), 1: ("ax-",), 2: ("a2",)}[rx])
    part_b = set(z_arrivals(k)) if rx == 0 else {{-1: f"x{k}+", 1: f"x{k}-", 2: f"y{k}"}[rx]}
    return part_a | part_b


EXPECTED = {
    "z1": 6.0, "z2": 7.0, "ax": 6.2, "a2": 6.6, "x0": 8.0, "z3": 10.0, "z4": 11.0, "az1": 10.2, "az2": 11.2, "x-1": 9.0, "x1": 9.0,
    "x-2": 12.0, "x2": 12.0, "az3": 14.0, "az4": 15.0, "x-3": 15.0, "x3": 15.0, "x4": 16.0, "y0": 12.5, "y-1": 14.5, "y1": 14.5,
    "y-2": 17.0, "y2": 17.0, "y-3": 20.0, "y3": 20.0, "y4": 21.0, "s0": 13.0, "sa": 16.5, "s-1": 18.0, "s1": 18.0,
}


def expected(name):
    if name.startswith("sy"):
        return EXPECTED[name[1:]] + 2.0
    return EXPECTED[name.rstrip("+-") if name not in EXPECTED else name]


def event_order(table):
    started, seen, order = set(), set(), []

    def start():
        ready = [i for i, entry in enumerate(table) if i not in started and all(q in seen for q in entry[4])]
        for i in sorted(ready, key=lambda i: (table[i][1][0] == "s", i)):
            order.append(i)
            started.add(i)

    start()
    for i in sorted(range(len(table)), key=lambda i: (expected(table[i][0]), i)):
        order.append(~i)
        seen.add(table[i][0])
        start()
    return order


COPIES = len(transfers())


class Gather:
    def __init__(self, mine, blocks, send_sem, recv_sem):
        self.mine, self.blocks, self.send_sem, self.recv_sem = mine, blocks, send_sem, recv_sem
        v, self.y = lax.axis_index("vol"), lax.axis_index("slab")
        self.x, self.z, self.c = v // (2 * NZ), (v // 2) % NZ, v % 2
        self.table = transfers()
        self.order = event_order(self.table)

    def place(self, direction, way=1):
        kind, d = direction
        if kind == "x":
            return (self.x + way * d + NX) % NX, self.z, self.c
        if kind == "z":
            return self.x, (self.z + way * d + NZ) % NZ, self.c
        return self.x, self.z, 1 - self.c

    def device(self, direction, way=1):
        x, z, c = self.place(direction, way)
        return ((x * NZ + z) * 2 + c, self.y)

    def at(self, spec, x, z, core, rows):
        kind, rx, rz = spec
        x, z, r = (x + rx + NX) % NX, (z + rz + NZ) % NZ, pl.ds(*rows)
        if kind == "x_all":
            return self.blocks.at[:, z, core, r]
        if kind == "x_low":
            return self.blocks.at[pl.ds(0, 2), z, core, r]
        if kind == "x_high":
            return self.blocks.at[pl.ds(2, 2), z, core, r]
        if kind == "z_all":
            return self.blocks.at[x, :, core, r]
        if kind == "all":
            return self.blocks.at[:, :, core, r]
        return self.blocks.at[x, z, core, r]

    def copy(self, i, arriving=False):
        _, direction, spec, rows, after = self.table[i]
        if arriving:
            source = target = self.at(spec, *self.place(direction, -1), rows)
        else:
            target = self.at(spec, self.x, self.z, self.c, rows)
            source = target if after else self.mine.at[pl.ds(*rows)]
        return pltpu.make_async_remote_copy(
            src_ref=source, dst_ref=target, send_sem=self.send_sem.at[i], recv_sem=self.recv_sem.at[i],
            device_id=self.device(direction), device_id_type=MESH)

    def greet(self, others):
        barrier = pltpu.get_barrier_semaphore()
        directions = list(dict.fromkeys(entry[1] for entry in self.table))
        for direction in directions:
            pl.semaphore_signal(barrier, inc=1, device_id=self.device(direction, -1), device_id_type=MESH)
        for peer in others:
            pl.semaphore_signal(barrier, inc=1, device_id=peer, device_id_type=MESH)
        return lambda: pl.semaphore_wait(barrier, len(directions) + len(others))

    def leave(self):
        for i in range(COPIES):
            self.copy(i).wait_send()


ANY = pl.BlockSpec(memory_space=pl.ANY)
VM = pl.BlockSpec(memory_space=pltpu.VMEM)


def owner_force(x, z, core, table, blocks_ref, sorted_ref, segment_ref):
    owner = (x * NZ + z) * 2 + core
    first = jnp.clip(table[0, owner], 0, sorted_ref.shape[0] - CAP)
    offset = blocks_ref[x, z, core, 64:72, :].astype(F32)[0:1]
    rows = sorted_ref[pl.ds(first, CAP), :].astype(BF16)
    masks = segment_masks(segment_ref[pl.ds(first, CAP), :])
    every = dot(rows[:, 0:64], blocks_ref[x, z, core, 0:64, :])
    gap = jnp.zeros((CAP, 128), F32)
    for p in range(4):
        at = slice(128 * p, 128 * p + 128)
        gap = jnp.where(masks[p], every[:, at] - offset[:, at], gap)
    traction = jnp.maximum(-gap, 0.0) + jnp.log(1.0 + jnp.exp(-jnp.abs(gap)))
    parts = [jnp.concatenate([jnp.where(m, part.astype(F32), 0.0) for m in masks], axis=1) for part in split(traction)]
    force = dot_nt(jnp.concatenate(parts, axis=0).astype(BF16), blocks_ref[x, z, core, 0:64, :])
    held = jnp.where(iota((1, CAP), 1) < table[1, owner], 1.0, 0.0)
    return rows, (force[:CAP] + force[CAP:]).astype(BF16), held


def spread_faces(found, shape_ref, total_ref):
    rows, force, held = (jnp.concatenate(part, axis=axis) for part, axis in zip(zip(*found), (0, 0, 1)))
    choose = hot(iota((16, 128), 1) == iota((16, 128), 0) + 64)
    extra = dot_nt(choose, rows)
    area = (extra[8:9] + extra[9:10] + extra[10:11]) * held
    s_high, s_low = split(shape_ref[...])
    nodal = dot_nt(jnp.concatenate([s_high.astype(F32), s_low.astype(F32)], axis=0).astype(BF16), force)
    nodal = (nodal[:12] + nodal[12:]) * area
    total_ref[...] = scatter_faces(nodal, extra[0:4].astype(I32), extra[4:8].astype(I32), total_ref[...])


def kernel(*refs):
    inputs, out_ref, buffers = refs[:12], refs[12], refs[13:25]
    blocks_ref, sorted_ref, segment_ref, mine, low_ref, total_ref, table_ref, rims, came, table = refs[25:35]
    load_sem, own_sem, send_sem, recv_sem, rim_send, rim_recv = refs[35:]
    slabs = lax.axis_size("slab")
    gather = Gather(mine, blocks_ref, send_sem, recv_sem)
    v, y = lax.axis_index("vol"), gather.y
    peers = ((v, (y + 1) % slabs), (v, (y + slabs - 1) % slabs))
    enter = gather.greet(peers)
    loads = [pltpu.make_async_copy(s, d, load_sem.at[k]) for k, (s, d) in enumerate(zip(inputs, buffers))]
    for load in loads:
        load.start()
    mortar, offset, owner, disp, segment, area, nodes, node, stiffness, connect, matrix, shape = buffers
    loads[0].wait()
    loads[1].wait()
    eye = hot(iota((64, 64), 0) == iota((64, 64), 1))
    mine[0:64, :] = dot_nt(eye, mortar[...].reshape(512, 64)).astype(BF16)
    gaps = offset[...].astype(F32)
    line = jnp.concatenate([gaps[g : g + 1] for g in range(8)], axis=1)
    mine[64:72, :] = jnp.broadcast_to(line, (8, 512)).astype(BF16)
    own = pltpu.make_async_copy(mine, gather.at(("one", 0, 0), gather.x, gather.z, gather.c, (0, BLOCK)), own_sem.at[0])
    own.start()
    enter()
    first_wait = next(i for i, e in enumerate(gather.order) if e < 0)
    for e in gather.order[:first_wait]:
        gather.copy(e).start()
    for load in loads[2:]:
        load.wait()
    total_ref[...] = jnp.zeros_like(total_ref)
    row, count, first = sort_faces(owner[...], 64)
    table_ref[...] = owner_table(first, count)
    to_smem = pltpu.make_async_copy(table_ref, table, own_sem.at[1])
    to_smem.start()
    content = jnp.concatenate(face_content(disp[...], segment[...], area[...], nodes[...]), axis=0)
    sorted_ref[2048:, :] = jnp.zeros((CAP, 128), F32)
    segment_ref[2048:, :] = jnp.zeros((CAP, 128), F32)
    own.wait()
    to_smem.wait()

    def owners(core, rx, ks):
        found = []
        for k in ks:
            z = (gather.z + k + NZ) % NZ
            x = (gather.x + rx + NX) % NX
            c = 1 - gather.c if core else gather.c
            found.append(owner_force(x, z, c, table, blocks_ref, sorted_ref, segment_ref))
        spread_faces(found, shape, total_ref)

    work = [(set(), lambda k=k: permute_rows(k, row, content, sorted_ref, segment_ref)) for k in range(8)]
    early = {"z1+", "z1-", "z2+", "z2-", "ax+", "ax-", "a2", "x0+", "x0-"}
    late = {"z3+", "z3-", "z4+", "z4-", "az1+", "az1-", "az2+", "az2-"}
    work.append((early, lambda: elements(node[...], connect[...], stiffness[...], matrix[...], total_ref, low_ref)))
    for core in (0, 1):
        for rx in (0, -1, 1, 2):
            for ks in ((0, -1, 1, -2), (2, -3, 3, 4)):
                need = set().union(*[needed(core, rx, k) for k in ks]) | late
                work.append((need, lambda core=core, rx=rx, ks=ks: owners(core, rx, ks)))
    seen = set()

    def do(budget):
        for _ in range(budget):
            for i, (need, piece) in enumerate(work):
                if need <= seen:
                    work.pop(i)
                    piece()
                    break
            else:
                return

    do(BEFORE_FIRST_WAIT)
    for e in gather.order[first_wait:]:
        if e >= 0:
            gather.copy(e).start()
            continue
        gather.copy(~e, True).wait_recv()
        seen.add(gather.table[~e][0])
        do(1)
    do(len(work))
    assert not work
    gather.leave()
    total = total_ref[...]
    grids = [total[16 * c : 16 * c + 8] + total[16 * c + 8 : 16 * c + 16] for c in range(3)]
    for c in range(3):
        rims[8 * c : 8 * c + 8] = grids[c]
    copies = [
        pltpu.make_async_remote_copy(
            src_ref=rims, dst_ref=came.at[k], send_sem=rim_send.at[k], recv_sem=rim_recv.at[k], device_id=peer, device_id_type=MESH)
        for k, peer in enumerate(peers)
    ]
    for copy in copies:
        copy.start()
    for copy in copies:
        copy.wait()
    for c in range(3):
        for h in range(8):
            line = grids[c][h : h + 1]
            if h < 2:
                line = line + jnp.where(y > 0, came[0, 8 * c + h + 6 : 8 * c + h + 7], 0.0)
            if h >= 6:
                line = line + jnp.where(y < slabs - 1, came[1, 8 * c + h - 6 : 8 * c + h - 5], 0.0)
            out_ref[c : c + 1, 128 * h : 128 * h + 128] = line


BEFORE_FIRST_WAIT = 8


def shards(face_disp, contact_owner, segment, face_area, face_nodes, mortar_blocks, gap_offset, shape_table, node_disp, stiffness, connect, elem_matrix):
    arrays = (
        mortar_blocks, gap_offset, contact_owner.reshape(1, 2048), face_disp, segment.reshape(1, 2048),
        face_area.reshape(1, 2048), face_nodes, node_disp, stiffness.reshape(1, 1024), connect, elem_matrix, shape_table)
    return pl.pallas_call(
        kernel,
        out_shape=jax.ShapeDtypeStruct((3, 1024), F32),
        in_specs=[ANY] * 12,
        out_specs=VM,
        scratch_shapes=[pltpu.VMEM(a.shape, a.dtype) for a in arrays]
        + [
            pltpu.VMEM((NX, NZ, 2, BLOCK, 512), BF16),
            pltpu.VMEM((2048 + CAP, 128), F32),
            pltpu.VMEM((2048 + CAP, 128), F32),
            pltpu.VMEM((BLOCK, 512), BF16),
            pltpu.VMEM((8, 128, 1024), BF16),
            pltpu.VMEM((48, 128), F32),
            pltpu.VMEM((8, 128), I32),
            pltpu.VMEM((24, 128), F32),
            pltpu.VMEM((2, 24, 128), F32),
            pltpu.SMEM((8, 128), I32),
            pltpu.SemaphoreType.DMA((12,)),
            pltpu.SemaphoreType.DMA((2,)),
            pltpu.SemaphoreType.DMA((COPIES,)),
            pltpu.SemaphoreType.DMA((COPIES,)),
            pltpu.SemaphoreType.DMA((2,)),
            pltpu.SemaphoreType.DMA((2,)),
        ],
        compiler_params=pltpu.CompilerParams(collective_id=0, has_side_effects=True, vmem_limit_bytes=60 << 20),
        name="contact_residual",
    )(*arrays)


def solution(mesh):
    both = ("vol", "slab")
    in_specs = (
        P(None, both), P(both, None), P(both), P(both), P(None, both), P(both, None, None), P(both, None), P(),
        P(None, both), P(both), P(None, both), P())
    return jax.shard_map(shards, mesh=mesh, in_specs=in_specs, out_specs=P(None, both), check_vma=False)
```

```python
import functools

import jax
import jax.numpy as jnp
from jax import lax
from jax.experimental import pallas as pl
from jax.experimental.pallas import tpu as pltpu
from jax.sharding import PartitionSpec as P

SH = 256
TILE = 32
CAP = 128
F32, BF16, I32 = jnp.float32, jnp.bfloat16, jnp.int32
NT = (((1,), (1,)), ((), ()))


def dot(a, b):
    return jnp.dot(a, b, preferred_element_type=F32)


def dot_nt(a, b):
    return lax.dot_general(a, b, NT, preferred_element_type=F32)


def iota(shape, dim):
    return lax.broadcasted_iota(I32, shape, dim)


def hot(mask):
    return jnp.where(mask, 1.0, 0.0).astype(BF16)


def split(value):
    high = value.astype(BF16)
    return high, (value - high.astype(F32)).astype(BF16)


def sort_faces(owner, owners):
    faces = owner.shape[1]
    member = iota((owners, faces), 0) == owner
    member_low = hot(member)
    upto = hot(iota((256, 256), 0) <= iota((256, 256), 1))
    carry = jnp.zeros((owners, 1), F32)
    parts = []
    for k in range(faces // 256):
        part = dot(member_low[:, 256 * k : 256 * k + 256], upto) + carry
        carry = part[:, 255:256]
        parts.append(part)
    rank = jnp.concatenate(parts, axis=1)
    before = hot(iota((owners, owners), 1) < iota((owners, owners), 0))
    count = jnp.broadcast_to(carry, (owners, 128))
    first = dot(before, count.astype(BF16))
    row = jnp.sum(jnp.where(member, rank - 1.0 + first[:, 0:1], 0.0), axis=0, keepdims=True)
    return row.astype(I32), count, first


def owner_table(first, count):
    owners = first.shape[0]
    mine = iota((owners, 128), 0) == iota((owners, 128), 1)
    lines = [jnp.sum(jnp.where(mine, value, 0.0), axis=0, keepdims=True) for value in (first, count)]
    return jnp.concatenate(lines + [jnp.zeros((6, 128), F32)], axis=0).astype(I32)


def face_content(disp, segment, area, nodes):
    faces = disp.shape[1]
    nodes_high = nodes >> 7
    area_a = area.astype(BF16)
    area_b, area_c = split(area - area_a.astype(F32))
    extra = jnp.concatenate([(nodes - (nodes_high << 7)).astype(F32), nodes_high.astype(F32)], axis=0).astype(BF16)
    return [
        disp,
        extra,
        area_a,
        area_b,
        area_c,
        jnp.zeros((53, faces), BF16),
        jnp.broadcast_to(segment.astype(F32), (128, faces)).astype(BF16),
    ]


def permute_rows(k, row, content, sorted_ref, segment_ref):
    pick = hot(iota((256, row.shape[1]), 0) + 256 * k == row)
    part = dot_nt(pick, content)
    sorted_ref[256 * k : 256 * k + 256, :] = part[:, 0:128]
    segment_ref[256 * k : 256 * k + 256, :] = part[:, 128:256] - (iota((256, 128), 1) >= 64).astype(F32)


def high_hot(high_row):
    return iota((8, high_row.shape[1]), 0) == high_row


def elements(node, connect, stiffness, matrix, total_ref, low_ref):
    count = connect.shape[1]
    rows = []
    for c in range(3):
        grid = jnp.concatenate([node[c : c + 1, 128 * h : 128 * h + 128] for h in range(8)], axis=0)
        high, low = split(grid)
        rows += [high.astype(F32), low.astype(F32)]
    table = jnp.concatenate(rows, axis=0).astype(BF16)
    picked, highs = [], []
    for a in range(8):
        index = connect[a : a + 1, :]
        high = index >> 7
        low = hot(iota((128, count), 0) == index - (high << 7))
        low_ref[a] = low
        mask = high_hot(high)
        highs.append(mask)
        got = dot(table, low)
        picked.append(jnp.concatenate([jnp.where(mask, got[8 * i : 8 * i + 8], 0.0) for i in range(6)], axis=0).astype(BF16))
    spread = hot(iota((24, 384), 1) // 16 == iota((24, 384), 0))
    m_high, m_low = split(matrix)
    wide = jnp.concatenate([dot(m_high, spread), dot(m_low, spread)], axis=0).astype(BF16)
    force = dot(wide, jnp.concatenate(picked, axis=0))
    force = (force[:24] + force[24:]) * stiffness
    total = jnp.zeros((48, 128), F32)
    for a in range(8):
        parts = []
        for c in range(3):
            for part in split(force[3 * a + c : 3 * a + c + 1]):
                parts.append(jnp.where(highs[a], part.astype(F32), 0.0))
        total = total + dot_nt(jnp.concatenate(parts, axis=0).astype(BF16), low_ref[a])
    total_ref[...] += total


def scatter_faces(nodal, low_rows, high_rows, total):
    count = nodal.shape[1]
    for a in range(4):
        low = hot(iota((128, count), 0) == low_rows[a : a + 1])
        mask = high_hot(high_rows[a : a + 1])
        parts = []
        for c in range(3):
            for part in split(nodal[3 * a + c : 3 * a + c + 1]):
                parts.append(jnp.where(mask, part.astype(F32), 0.0))
        total = total - dot_nt(jnp.concatenate(parts, axis=0).astype(BF16), low)
    return total


def segment_masks(segment):
    return [segment == 2.0 * p for p in range(4)]


NX, NZ = 4, 8
MESH = pl.DeviceIdType.MESH
BLOCK = 72
A, B = (0, 16), (16, 56)
B0, B1 = (16, 24), (40, 32)
RING = (0, -1, 1, -2, 2, -3, 3, 4)


def sign(d):
    return "+" if d > 0 else "-"


def transfers():
    t = []

    def add(*entry):
        t.append(entry)

    for d in (1, -1):
        add("z1" + sign(d), ("z", d), ("one", 0, 0), B, ())
        add("z2" + sign(d), ("z", 2 * d), ("one", 0, 0), B, ())
    for d in (1, -1):
        add("ax" + sign(d), ("x", d), ("one", 0, 0), A, ())
    add("a2", ("x", 2), ("one", 0, 0), A, ())
    for d in (1, -1):
        add("z3" + sign(d), ("z", 2 * d), ("one", 0, -d), B, ("z1" + sign(d),))
        add("z4" + sign(d), ("z", 2 * d), ("one", 0, -2 * d), B0 if d > 0 else B1, ("z2" + sign(d),))
    a_line = ("ax+", "ax-", "a2")
    for d in (1, -1):
        add("az1" + sign(d), ("z", d), ("x_all", 0, 0), A, a_line)
        add("az2" + sign(d), ("z", 2 * d), ("x_all", 0, 0), A, a_line)
    for k in RING:
        for d in (1, -1):
            add(f"x{k}" + sign(d), ("x", d), ("one", 0, k), B, z_arrivals(k))
    for d in (1, -1):
        add("az3" + sign(d), ("z", 2 * d), ("x_all", 0, -d), A, ("az1" + sign(d),))
        add("az4" + sign(d), ("z", 2 * d), ("x_low" if d > 0 else "x_high", 0, -2 * d), A, ("az2" + sign(d),))
    for k in RING:
        d = 1 if k in (0, 1, 2, 3) else -1
        add(f"y{k}", ("x", d), ("one", -d, k), B, (f"x{k}" + sign(d),))
    return t


def z_arrivals(k):
    if k == 0:
        return ()
    if k == 4:
        return ("z4+", "z4-")
    return (f"z{abs(k)}" + sign(-k),)


def az_arrivals(k):
    return tuple("a" + q for q in z_arrivals(k))


def needed(rx, k):
    part_a = set(az_arrivals(k)) if k else set({0: (), -1: ("ax+",), 1: ("ax-",), 2: ("a2",)}[rx])
    part_b = set(z_arrivals(k)) if rx == 0 else {{-1: f"x{k}+", 1: f"x{k}-", 2: f"y{k}"}[rx]}
    return part_a | part_b


EXPECTED = {
    "z1": 9.0, "z2": 10.5, "ax": 7.5, "a2": 8.5, "x0": 9.0, "z3": 13.5, "z4": 14.5, "az1": 12.5, "az2": 13.5, "x-1": 12.6, "x1": 12.6,
    "x-2": 14.6, "x2": 14.8, "az3": 17.0, "az4": 17.5, "x-3": 18.0, "x3": 18.2, "x4": 20.0, "y0": 12.8, "y-1": 16.0, "y1": 16.2,
    "y-2": 19.0, "y2": 19.2, "y-3": 22.0, "y3": 22.2, "y4": 23.5,
}


def expected(name):
    return EXPECTED[name.rstrip("+-") if name not in EXPECTED else name]


def event_order(table):
    started, seen, order = set(), set(), []

    def start():
        ready = [i for i, entry in enumerate(table) if i not in started and all(q in seen for q in entry[4])]
        for i in sorted(ready, key=lambda i: (table[i][1][0] == "s", i)):
            order.append(i)
            started.add(i)

    start()
    for i in sorted(range(len(table)), key=lambda i: (expected(table[i][0]), i)):
        order.append(~i)
        seen.add(table[i][0])
        start()
    return order


COPIES = len(transfers())


class Gather:
    def __init__(self, mine, blocks, send_sem, recv_sem):
        self.mine, self.blocks, self.send_sem, self.recv_sem = mine, blocks, send_sem, recv_sem
        v, self.y = lax.axis_index("vol"), lax.axis_index("slab")
        self.x, self.z, self.c = v // (2 * NZ), (v // 2) % NZ, v % 2
        self.table = transfers()
        self.order = event_order(self.table)

    def place(self, direction, way=1):
        kind, d = direction
        if kind == "x":
            return (self.x + way * d + NX) % NX, self.z, self.c
        if kind == "z":
            return self.x, (self.z + way * d + NZ) % NZ, self.c
        return self.x, self.z, 1 - self.c

    def device(self, direction, way=1):
        x, z, c = self.place(direction, way)
        return ((x * NZ + z) * 2 + c, self.y)

    def at(self, spec, x, z, core, rows):
        kind, rx, rz = spec
        x, z, r = (x + rx + NX) % NX, (z + rz + NZ) % NZ, pl.ds(*rows)
        if kind == "x_all":
            return self.blocks.at[:, z, r]
        if kind == "x_low":
            return self.blocks.at[pl.ds(0, 2), z, r]
        if kind == "x_high":
            return self.blocks.at[pl.ds(2, 2), z, r]
        return self.blocks.at[x, z, r]

    def copy(self, i, arriving=False):
        _, direction, spec, rows, after = self.table[i]
        if arriving:
            source = target = self.at(spec, *self.place(direction, -1), rows)
        else:
            target = self.at(spec, self.x, self.z, self.c, rows)
            source = target if after else self.mine.at[pl.ds(*rows)]
        return pltpu.make_async_remote_copy(
            src_ref=source, dst_ref=target, send_sem=self.send_sem.at[i], recv_sem=self.recv_sem.at[i],
            device_id=self.device(direction), device_id_type=MESH)

    def greet(self, others):
        barrier = pltpu.get_barrier_semaphore()
        directions = list(dict.fromkeys(entry[1] for entry in self.table))
        for direction in directions:
            pl.semaphore_signal(barrier, inc=1, device_id=self.device(direction, -1), device_id_type=MESH)
        for peer in others:
            pl.semaphore_signal(barrier, inc=1, device_id=peer, device_id_type=MESH)
        return lambda: pl.semaphore_wait(barrier, len(directions) + len(others))

    def leave(self):
        for i in range(COPIES):
            self.copy(i).wait_send()


ANY = pl.BlockSpec(memory_space=pl.ANY)
VM = pl.BlockSpec(memory_space=pltpu.VMEM)


def owner_force(x, z, core, faces, blocks_ref):
    owner = (x * NZ + z) * 2 + core
    offset = blocks_ref[x, z, 64:72, :].astype(F32)[0:1]
    at = [pl.ds(jnp.clip(table[0, owner], 0, sorted_ref.shape[0] - CAP), CAP) for sorted_ref, _, table, _ in faces]
    rows = [f[0][a, :].astype(BF16) for f, a in zip(faces, at)]
    masks = segment_masks(jnp.concatenate([f[1][a, :] for f, a in zip(faces, at)], axis=0))
    every = dot(jnp.concatenate(rows, axis=0)[:, 0:64], blocks_ref[x, z, 0:64, :])
    gap = jnp.zeros((len(faces) * CAP, 128), F32)
    for p in range(4):
        cut = slice(128 * p, 128 * p + 128)
        gap = jnp.where(masks[p], every[:, cut] - offset[:, cut], gap)
    traction = jnp.maximum(-gap, 0.0) + jnp.log(1.0 + jnp.exp(-jnp.abs(gap)))
    parts = [jnp.concatenate([jnp.where(m, part.astype(F32), 0.0) for m in masks], axis=1) for part in split(traction)]
    force = dot_nt(jnp.concatenate(parts, axis=0).astype(BF16), blocks_ref[x, z, 0:64, :])
    force = (force[: len(faces) * CAP] + force[len(faces) * CAP :]).astype(BF16)
    held = [jnp.where(iota((1, CAP), 1) < f[2][1, owner], 1.0, 0.0) for f in faces]
    return [(rows[k], force[CAP * k : CAP * k + CAP], held[k]) for k in range(len(faces))]


def spread_faces(found, shape_ref, total_ref):
    rows, force, held = (jnp.concatenate(part, axis=axis) for part, axis in zip(zip(*found), (0, 0, 1)))
    choose = hot(iota((16, 128), 1) == iota((16, 128), 0) + 64)
    extra = dot_nt(choose, rows)
    area = (extra[8:9] + extra[9:10] + extra[10:11]) * held
    s_high, s_low = split(shape_ref[...])
    nodal = dot_nt(jnp.concatenate([s_high.astype(F32), s_low.astype(F32)], axis=0).astype(BF16), force)
    nodal = (nodal[:12] + nodal[12:]) * area
    total_ref[...] = scatter_faces(nodal, extra[0:4].astype(I32), extra[4:8].astype(I32), total_ref[...])


def kernel(*refs):
    inputs, out_ref, buffers = refs[:12], refs[12], refs[13:25]
    blocks_ref, sorted_ref, segment_ref, sorted_two, segment_two, mine, low_ref, total_ref, total_two, total_came = refs[25:35]
    table_ref, table_came, rims, came, table, table_two = refs[35:41]
    load_sem, own_sem, send_sem, recv_sem, rim_send, rim_recv, share_send, share_recv = refs[41:]
    slabs = lax.axis_size("slab")
    gather = Gather(mine, blocks_ref, send_sem, recv_sem)
    v, y = lax.axis_index("vol"), gather.y
    peers = ((v, (y + 1) % slabs), (v, (y + slabs - 1) % slabs))
    twin = (v + 1 - 2 * gather.c, y)
    enter = gather.greet(peers + (twin,))
    loads = [pltpu.make_async_copy(s, d, load_sem.at[k]) for k, (s, d) in enumerate(zip(inputs, buffers))]
    for load in loads:
        load.start()
    mortar, offset, owner, disp, segment, area, nodes, node, stiffness, connect, matrix, shape = buffers
    loads[0].wait()
    loads[1].wait()
    eye = hot(iota((64, 64), 0) == iota((64, 64), 1))
    mine[0:64, :] = dot_nt(eye, mortar[...].reshape(512, 64)).astype(BF16)
    gaps = offset[...].astype(F32)
    line = jnp.concatenate([gaps[g : g + 1] for g in range(8)], axis=1)
    mine[64:72, :] = jnp.broadcast_to(line, (8, 512)).astype(BF16)
    own = pltpu.make_async_copy(mine, gather.at(("one", 0, 0), gather.x, gather.z, gather.c, (0, BLOCK)), own_sem.at[0])
    own.start()
    enter()
    first_wait = next(i for i, e in enumerate(gather.order) if e < 0)
    for e in gather.order[:first_wait]:
        gather.copy(e).start()
    for load in loads[2:]:
        load.wait()
    total_ref[...] = jnp.zeros_like(total_ref)
    row, count, first = sort_faces(owner[...], 64)
    table_ref[...] = owner_table(first, count)
    to_smem = pltpu.make_async_copy(table_ref, table, own_sem.at[1])
    to_smem.start()
    content = jnp.concatenate(face_content(disp[...], segment[...], area[...], nodes[...]), axis=0)
    sorted_ref[2048:, :] = jnp.zeros((CAP, 128), F32)
    segment_ref[2048:, :] = jnp.zeros((CAP, 128), F32)
    own.wait()
    to_smem.wait()
    for k in range(8):
        permute_rows(k, row, content, sorted_ref, segment_ref)
    shared = [
        pltpu.make_async_remote_copy(
            src_ref=source, dst_ref=target, send_sem=share_send.at[k], recv_sem=share_recv.at[k], device_id=twin, device_id_type=MESH)
        for k, (source, target) in enumerate(
            ((table_ref, table_came), (sorted_ref, sorted_two), (segment_ref, segment_two), (total_two, total_came)))
    ]
    for copy in shared[:3]:
        copy.start()
    total_two[...] = jnp.zeros_like(total_two)
    faces = ((sorted_ref, segment_ref, table, total_ref), (sorted_two, segment_two, table_two, total_two))

    def receive():
        for copy in shared[:3]:
            copy.wait()
        move = pltpu.make_async_copy(table_came, table_two, own_sem.at[1])
        move.start()
        move.wait()

    def owners(rx, ks):
        found = []
        for k in ks:
            z = (gather.z + k + NZ) % NZ
            x = (gather.x + rx + NX) % NX
            found.append(owner_force(x, z, gather.c, faces, blocks_ref))
        for k in range(2):
            spread_faces([f[k] for f in found], shape, faces[k][3])

    early = {"z1+", "z1-", "z2+", "z2-", "ax+", "ax-", "a2"}
    work = [(early, ELEMENTS_US, lambda: elements(node[...], connect[...], stiffness[...], matrix[...], total_ref, low_ref))]
    work.append((early, 0.3, receive))
    for rx in (0, -1, 1, 2):
        for ks in ((0, -1, 1, -2), (2, -3, 3, 4)):
            need = set().union(*[needed(rx, k) for k in ks]) | early
            work.append((need, OWNERS_US, lambda rx=rx, ks=ks: owners(rx, ks)))
    seen = set()

    def do(room):
        used = 0.0
        while True:
            for i, (need, cost, piece) in enumerate(work):
                if need <= seen and used + cost <= room:
                    work.pop(i)
                    piece()
                    used += cost
                    break
            else:
                return used

    clock = FIRST_WAIT_US
    for e in gather.order[first_wait:]:
        if e >= 0:
            gather.copy(e).start()
            clock += 0.05
            continue
        due = expected(gather.table[~e][0])
        clock += do(due + SLACK_US - clock)
        gather.copy(~e, True).wait_recv()
        clock = max(clock, due) + 0.05
        seen.add(gather.table[~e][0])
    do(1e9)
    assert not work
    shared[3].start()
    gather.leave()
    shared[3].wait()
    total_ref[...] += total_came[...]
    total = total_ref[...]
    grids = [total[16 * c : 16 * c + 8] + total[16 * c + 8 : 16 * c + 16] for c in range(3)]
    for c in range(3):
        rims[8 * c : 8 * c + 8] = grids[c]
    copies = [
        pltpu.make_async_remote_copy(
            src_ref=rims, dst_ref=came.at[k], send_sem=rim_send.at[k], recv_sem=rim_recv.at[k], device_id=peer, device_id_type=MESH)
        for k, peer in enumerate(peers)
    ]
    for copy in copies:
        copy.start()
    for copy in copies:
        copy.wait()
    for c in range(3):
        for h in range(8):
            line = grids[c][h : h + 1]
            if h < 2:
                line = line + jnp.where(y > 0, came[0, 8 * c + h + 6 : 8 * c + h + 7], 0.0)
            if h >= 6:
                line = line + jnp.where(y < slabs - 1, came[1, 8 * c + h - 6 : 8 * c + h - 5], 0.0)
            out_ref[c : c + 1, 128 * h : 128 * h + 128] = line


FIRST_WAIT_US, ELEMENTS_US, OWNERS_US, SLACK_US = 9.0, 2.5, 1.3, 100.0


def shards(face_disp, contact_owner, segment, face_area, face_nodes, mortar_blocks, gap_offset, shape_table, node_disp, stiffness, connect, elem_matrix):
    arrays = (
        mortar_blocks, gap_offset, contact_owner.reshape(1, 2048), face_disp, segment.reshape(1, 2048),
        face_area.reshape(1, 2048), face_nodes, node_disp, stiffness.reshape(1, 1024), connect, elem_matrix, shape_table)
    return pl.pallas_call(
        kernel,
        out_shape=jax.ShapeDtypeStruct((3, 1024), F32),
        in_specs=[ANY] * 12,
        out_specs=VM,
        scratch_shapes=[pltpu.VMEM(a.shape, a.dtype) for a in arrays]
        + [
            pltpu.VMEM((NX, NZ, BLOCK, 512), BF16),
            pltpu.VMEM((2048 + CAP, 128), F32),
            pltpu.VMEM((2048 + CAP, 128), F32),
            pltpu.VMEM((2048 + CAP, 128), F32),
            pltpu.VMEM((2048 + CAP, 128), F32),
            pltpu.VMEM((BLOCK, 512), BF16),
            pltpu.VMEM((8, 128, 1024), BF16),
            pltpu.VMEM((48, 128), F32),
            pltpu.VMEM((48, 128), F32),
            pltpu.VMEM((48, 128), F32),
            pltpu.VMEM((8, 128), I32),
            pltpu.VMEM((8, 128), I32),
            pltpu.VMEM((24, 128), F32),
            pltpu.VMEM((2, 24, 128), F32),
            pltpu.SMEM((8, 128), I32),
            pltpu.SMEM((8, 128), I32),
            pltpu.SemaphoreType.DMA((12,)),
            pltpu.SemaphoreType.DMA((2,)),
            pltpu.SemaphoreType.DMA((COPIES,)),
            pltpu.SemaphoreType.DMA((COPIES,)),
            pltpu.SemaphoreType.DMA((2,)),
            pltpu.SemaphoreType.DMA((2,)),
            pltpu.SemaphoreType.DMA((4,)),
            pltpu.SemaphoreType.DMA((4,)),
        ],
        compiler_params=pltpu.CompilerParams(collective_id=0, has_side_effects=True, vmem_limit_bytes=60 << 20),
        name="contact_residual",
    )(*arrays)


def solution(mesh):
    both = ("vol", "slab")
    in_specs = (
        P(None, both), P(both, None), P(both), P(both), P(None, both), P(both, None, None), P(both, None), P(),
        P(None, both), P(both), P(None, both), P())
    return jax.shard_map(shards, mesh=mesh, in_specs=in_specs, out_specs=P(None, both), check_vma=False)
```
